512 devices in a mesh: wave: 64 (over z, x_lo, core), lev: 8 (over y, x_hi).
Axes of the slice: x: 4 (x_hi: 2, x_lo: 2; x = x_hi * 2 + x_lo), y: 4, z: 16, core: 2. Of those that a mesh axis runs over, the one named last changes fastest.
Arguments:
- state: bfloat16 [72, 1280, 2560], P('lev', 'wave'), may hold values from -6 to 6
- panels: bfloat16 [512, 640, 1280], P(('wave', 'lev')), may hold values from -0.15625 to 0.15625
- pair_table: int32 [512], replicated, may hold values from 1 to 639, as said below
- lat_order: int32 [1280], replicated, may hold values from 0 to 1279, each once
- gauss_weights: float32 [1280], replicated, may hold values from 0.2 to 2
- eig: float32 [72], replicated, may hold values from 0.1 to 10
- left: bfloat16 [72, 72], replicated, may hold values from -0.75 to 0.75
- right: bfloat16 [72, 72], replicated, may hold values from -0.75 to 0.75
Outputs:
- new_state: bfloat16 [72, 1280, 2560], P('lev', 'wave')
- spectral: bfloat16 [512, 2, 72, 1280], P(('wave', 'lev'))
The draws below stay inside these ranges and needn't reach their ends.
Inputs may be any that keep to these rules, and one draw needn't show every extreme that they name: `pair_table`: 512 distinct numbers. `lat_order`: each latitude once.
All inputs are finite; a program needn't handle non-finite values.
Results may differ from the reference program's by a relative error of at most 0.012.
Values may be sent and summed in bfloat16 or wider, within the bound.
A program may use at most 64 MiB of HBM per device.

```python
import math
import jax
import jax.numpy as jnp
from jax import lax

NLON = 2560
NLAT = 1280
NCOL = 1280
LEV = 72
N_PAIRS = 512


def draw_pair_table(key, part):
    top = NCOL // 2 - 1
    middle = jax.random.permutation(key, top - 2).astype(jnp.int32) + 2
    chosen = jnp.concatenate([jnp.array([1, top], dtype=jnp.int32), middle[:N_PAIRS - 2]])
    return jax.random.permutation(jax.random.fold_in(key, 7), chosen).astype(jnp.int32)


def steps_of(stream_key, shape, split, smallest, high):
    def one(position, parts):
        steps = jax.random.uniform(jax.random.fold_in(jax.random.fold_in(stream_key, 6), position), (parts,), jnp.float32, smallest / len(split), high / len(split))
        return jnp.repeat(jnp.exp(steps), shape[position] // parts).reshape((-1,) + (1,) * (len(shape) - position - 1))

    level = one(*split[0])
    for cut in split[1:]:
        level = level * one(*cut)
    return level


def noise(stream_key, shape, spread, limit, split=(), kind=jnp.bfloat16):
    factor_of = steps_of(stream_key, shape, split, -0.22, 0.18) if split else 1.0
    values = jax.random.normal(stream_key, shape, jnp.float32) * spread * factor_of
    return jnp.minimum(jnp.maximum(values, -limit), limit).astype(kind)


def setup_inputs(seed: int = 0) -> dict:
    streams_of = jax.random.split(jax.random.key(seed), 9)
    state = noise(streams_of[0], (LEV, NLAT, NLON), 1.0, 6.0, ((0, 8), (1, 64)))
    panels = noise(streams_of[1], (N_PAIRS, NLAT // 2, NCOL), NLAT ** -0.5, 0.15625, ((0, 512),))
    pair_table = draw_pair_table(jax.random.fold_in(streams_of[8], 71), 0)
    lat_order = jax.random.permutation(streams_of[3], NLAT).astype(jnp.int32)
    gauss_weights = jnp.clip(jnp.exp(jax.random.uniform(streams_of[4], (NLAT,), jnp.float32, math.log(0.2), math.log(2.0))), 0.2, 2.0)
    eig = jnp.clip(jnp.exp(jax.random.uniform(streams_of[5], (LEV,), jnp.float32, math.log(0.1), math.log(10.0))), 0.1, 10.0)
    left = noise(streams_of[6], (LEV, LEV), LEV ** -0.5, 0.75)
    right = noise(streams_of[7], (LEV, LEV), LEV ** -0.5, 0.75)
    return {"state": state, "panels": panels, "pair_table": pair_table, "lat_order": lat_order, "gauss_weights": gauss_weights, "eig": eig, "left": left, "right": right}


def wave_values(firsts):
    seconds = NCOL - firsts
    waves = jnp.stack([firsts, firsts, seconds, seconds], axis=1).reshape(-1).astype(jnp.int32)
    points = jnp.arange(NLON, dtype=jnp.int32)
    phase = points[:, None] * waves[None, :] % NLON
    angle = phase.astype(jnp.float32) * (2.0 * math.pi / NLON)
    parity = jnp.arange(waves.shape[0], dtype=jnp.int32) % 2
    return jnp.where(parity[None, :] == 0, jnp.cos(angle), -jnp.sin(angle))

def mirror_signs(first):
    columns = jnp.arange(NCOL, dtype=jnp.int32)
    owned = columns < NCOL - first
    shifted = jnp.where(owned, columns, columns + first)
    return jnp.where(shifted % 2 == 0, 1.0, -1.0).astype(jnp.float32)

def pair_solve(panel, first, block, lat_order, eig, left, right):
    mirror = mirror_signs(first)
    half = panel.astype(jnp.float32)
    full = jnp.concatenate([half, mirror[None, :] * half[::-1]], axis=0)
    rows_panel = jnp.take(full, lat_order, axis=0)
    raw = jnp.einsum('kra,rc->kac', block.astype(jnp.float32), rows_panel)
    columns = jnp.arange(NCOL, dtype=jnp.int32)
    owned = columns < NCOL - first
    coeff = jnp.where(owned[None, None, :], raw[:, 0:2], raw[:, 2:4]).astype(jnp.bfloat16)
    degree = jnp.where(owned, columns + first, columns).astype(jnp.float32)
    factor = degree * (degree + 1.0) / (NCOL * (NCOL - 1.0))
    mixed = jnp.einsum('ji,iqc->jqc', right.astype(jnp.float32), coeff.astype(jnp.float32))
    scaled = (mixed / (1.0 + factor[None, None, :] * eig[:, None, None])).astype(jnp.bfloat16)
    solved = jnp.einsum('kj,jqc->kqc', left.astype(jnp.float32), scaled.astype(jnp.float32)).astype(jnp.bfloat16)
    zeros = jnp.zeros_like(solved)
    masked = jnp.concatenate([jnp.where(owned[None, None, :], solved, zeros), jnp.where(owned[None, None, :], zeros, solved)], axis=1)
    back = jnp.einsum('kac,rc->kra', masked.astype(jnp.float32), rows_panel).astype(jnp.bfloat16)
    return (jnp.transpose(solved, (1, 0, 2)), back)

def reference(state, panels, pair_table, lat_order, gauss_weights, eig, left, right):
    levels, rows, points = state.shape
    values = wave_values(pair_table)
    basis = (values * (1.0 / math.sqrt(NLON))).astype(jnp.bfloat16)
    flat = state.reshape(levels * rows, points)
    fourier = jnp.dot(flat, basis, preferred_element_type=jnp.float32).astype(jnp.bfloat16).reshape(levels, rows, -1)
    scale = jnp.take(gauss_weights, lat_order, axis=0)
    weighted = (fourier.astype(jnp.float32) * scale[None, :, None]).astype(jnp.bfloat16)
    blocks = jnp.transpose(weighted.reshape(levels, rows, N_PAIRS, 4), (2, 0, 1, 3))

    def one(items):
        panel, first, block = items
        return pair_solve(panel, first, block, lat_order, eig, left, right)
    spectral, back = lax.map(one, (panels, pair_table, blocks))
    joined = jnp.transpose(back, (1, 2, 0, 3)).reshape(levels * rows, -1)
    inverse = (jnp.transpose(values) * (2.0 / math.sqrt(NLON))).astype(jnp.bfloat16)
    new_state = jnp.dot(joined, inverse, preferred_element_type=jnp.float32).astype(jnp.bfloat16).reshape(state.shape)
    return (new_state, spectral)
```

```python
import math

import jax
import jax.numpy as jnp
import ml_dtypes
import numpy as np
from jax import lax
from jax.experimental import pallas as pl
from jax.experimental.pallas import tpu as pltpu
from jax.sharding import PartitionSpec as P

NLON = 2560
NCOL = 1280
HALF = 640
LEV = 72
LEVD = 9
ROWS = 20
PADR = 24
NZ = 16
NS = 32
CH = 3
NCH = LEVD // CH
MESH = pl.DeviceIdType.MESH
VM = pl.BlockSpec(memory_space=pltpu.VMEM)
SM = pl.BlockSpec(memory_space=pltpu.SMEM)
F32 = jnp.float32
BF = jnp.bfloat16
LIMIT = 56 * 1024 * 1024


def dft_table():
    x = np.arange(NLON // 2, dtype=np.int64)
    out = []
    for parity in (0, 1):
        m = 2 * np.arange(HALF, dtype=np.int64) + parity
        angle = (x[:, None] * m[None, :] % NLON) * (2.0 * math.pi / NLON)
        both = np.concatenate([np.cos(angle), -np.sin(angle)], axis=1)
        out.append(both * (1.0 / math.sqrt(NLON)))
    return np.stack(out).astype(np.float32).astype(ml_dtypes.bfloat16)


def lane_order():
    e = np.zeros((NS, 16, CH, 2, NS, 2), np.float32)
    for d in range(NS):
        for i in range(CH):
            for ab in range(2):
                for q in range(2):
                    e[d, i * 4 + ab * 2 + q, i, q, d, ab] = 1.0
    return e.reshape(NS * 16, CH * 128).astype(ml_dtypes.bfloat16)


def level_rows():
    o = np.zeros((4, LEV, NCH, 8, 16), np.float32)
    for c in range(NCH):
        for g in range(8):
            for i in range(CH):
                for j in range(4):
                    o[j, g * LEVD + c * CH + i, c, g, i * 4 + j] = 1.0
    return o.reshape(4, LEV, NCH * 128).astype(ml_dtypes.bfloat16)


def dot(a, b, ca=1, cb=0):
    return lax.dot_general(a, b, (((ca,), (cb,)), ((), ())), preferred_element_type=F32)


def one_hot(rows, columns, pos):
    return (lax.broadcasted_iota(jnp.int32, (rows, columns), 0) == pos).astype(F32).astype(BF)


def fourier_kernel(state_ref, table_ref, pos_ref, out_ref, pad, spec):
    pad[...] = jnp.zeros_like(pad)
    pad[:, :ROWS, :] = state_ref[...].astype(F32)
    flat = LEVD * PADR
    low = pad[:, :, : NLON // 2].reshape(flat, NLON // 2)
    high = pad[:, :, NLON // 2 :].reshape(flat, NLON // 2)
    for parity, part in ((0, low + high), (1, low - high)):
        both = dot(part.astype(BF), table_ref[parity]).astype(BF)
        spec[:flat, parity * HALF : (parity + 1) * HALF] = both[:, :HALF]
        spec[flat:, parity * HALF : (parity + 1) * HALF] = both[:, HALF:]
    left_half = lax.broadcasted_iota(jnp.int32, (flat, 128), 1) < 64
    for t in range(NZ // 2):
        pick = one_hot(NCOL, 128, pos_ref[:, t * 128 : (t + 1) * 128])
        got = dot(spec[...], pick)
        cos, sin = got[:flat], got[flat:]
        first = jnp.where(left_half, cos, pltpu.roll(sin, 64, 1))
        second = jnp.where(left_half, pltpu.roll(cos, 64, 1), sin)
        for h, value in ((0, first), (1, second)):
            columns = slice((2 * t + h) * 128, (2 * t + h + 1) * 128)
            out_ref[:, :, columns] = value.reshape(LEVD, PADR, 128)[:, :ROWS].astype(BF)


def inverse_kernel(in_ref, table_ref, pos_ref, out_ref, pad, pairs, spec):
    flat = LEVD * PADR
    pad[...] = jnp.zeros_like(pad)
    pad[:, :ROWS, :] = in_ref[...].astype(F32)
    left_half = lax.broadcasted_iota(jnp.int32, (flat, 128), 1) < 64
    for t in range(NZ // 2):
        first = pad[:, :, 2 * t * 128 : (2 * t + 1) * 128].reshape(flat, 128)
        second = pad[:, :, (2 * t + 1) * 128 : (2 * t + 2) * 128].reshape(flat, 128)
        columns = slice(t * 128, (t + 1) * 128)
        pairs[:flat, columns] = jnp.where(left_half, first, pltpu.roll(second, 64, 1)).astype(BF)
        pairs[flat:, columns] = jnp.where(left_half, pltpu.roll(first, 64, 1), second).astype(BF)
    for t in range(NCOL // 128):
        rows = lax.broadcasted_iota(jnp.int32, (128, NZ * 64), 0) + t * 128
        pick = (rows == pos_ref[...]).astype(F32).astype(BF)
        got = dot(pairs[...], pick, 1, 1).astype(BF)
        parity, k = divmod(t * 128, HALF)
        spec[parity, :, k : k + 128] = got[:flat]
        spec[parity, :, HALF + k : HALF + k + 128] = got[flat:]
    for t in range(NLON // 2 // 256):
        columns = slice(t * 256, (t + 1) * 256)
        even = dot(spec[0], table_ref[0, columns, :], 1, 1)
        odd = dot(spec[1], table_ref[1, columns, :], 1, 1)
        low = 2.0 * (even + odd)
        high = 2.0 * (even - odd)
        out_ref[:, :, columns] = low.reshape(LEVD, PADR, 256)[:, :ROWS].astype(BF)
        columns = slice(NLON // 2 + t * 256, NLON // 2 + (t + 1) * 256)
        out_ref[:, :, columns] = high.reshape(LEVD, PADR, 256)[:, :ROWS].astype(BF)


def place():
    wave, group = lax.axis_index("wave"), lax.axis_index("lev")
    z, s = wave // 4, lax.rem(wave, 4)

    def along_z(k):
        other = lax.rem(z + k, NZ)
        return other, (other * 4 + s, group)

    me = s * 8 + group

    def in_plane(k):
        other = lax.rem(me + k, NS)
        return other, (z * 4 + other // 8, lax.rem(other, 8))

    return z, along_z, me, in_plane


def greet(along_z, in_plane):
    barrier = pltpu.get_barrier_semaphore()

    def hail(of):
        def one(k, carry):
            pl.semaphore_signal(barrier, inc=1, device_id=of(k)[1], device_id_type=MESH)
            return carry

        return one

    lax.fori_loop(1, NZ, hail(along_z), 0)
    lax.fori_loop(1, NS, hail(in_plane), 0)
    pl.semaphore_wait(barrier, NZ - 1 + NS - 1)


def each(count, act):
    def one(k, carry):
        act(k)
        return carry

    lax.fori_loop(1, count, one, 0)


def lanes(z):
    return pl.ds(pl.multiple_of(z * 128, 128), 128)


def to_pairs_kernel(in_ref, order_ref, out_ref, got, ready, pad, zs, zr, ps, pr, own_z, own_p):
    z, along_z, me, in_plane = place()
    greet(along_z, in_plane)

    def z_copy(c, k):
        other, device = along_z(k)
        return pltpu.make_async_remote_copy(
            src_ref=in_ref.at[c * CH : (c + 1) * CH, :, lanes(other)],
            dst_ref=got.at[c * CH : (c + 1) * CH, z],
            send_sem=zs.at[c, k],
            recv_sem=zr.at[c, k],
            device_id=device,
            device_id_type=MESH,
        )

    def p_copy(c, k):
        other, device = in_plane(k)
        return pltpu.make_async_remote_copy(
            src_ref=ready.at[c, other],
            dst_ref=out_ref.at[c, me],
            send_sem=ps.at[c, k],
            recv_sem=pr.at[c, k],
            device_id=device,
            device_id_type=MESH,
        )

    mine = []
    for c in range(NCH):
        each(NZ, lambda k: z_copy(c, k).start())
        copy = pltpu.make_async_copy(
            in_ref.at[c * CH : (c + 1) * CH, :, lanes(z)],
            got.at[c * CH : (c + 1) * CH, z],
            own_z.at[c],
        )
        copy.start()
        mine.append(copy)
    pad[...] = jnp.zeros_like(pad)
    last = []
    for c in range(NCH):
        mine[c].wait()
        each(NZ, lambda k: z_copy(c, k).wait_recv())
        for i in range(CH):
            pad[i, :, :ROWS, :] = got[c * CH + i].astype(F32)
        block = jnp.concatenate(
            [pad[i].reshape(NZ * PADR, 128).astype(BF) for i in range(CH)], axis=1
        )
        ready[c] = dot(order_ref[...], block, 1, 1).astype(BF).reshape(NS, 16, NZ * PADR)
        each(NS, lambda k: p_copy(c, k).start())
        copy = pltpu.make_async_copy(ready.at[c, me], out_ref.at[c, me], own_p.at[c])
        copy.start()
        last.append(copy)
    for c in range(NCH):
        last[c].wait()
        each(NS, lambda k: p_copy(c, k).wait())
        each(NZ, lambda k: z_copy(c, k).wait_send())


def to_rows_kernel(in_ref, order_ref, out_ref, got, ready, zs, zr, ps, pr, own_z, own_p):
    z, along_z, me, in_plane = place()
    greet(along_z, in_plane)

    def z_copy(c, k):
        other, device = along_z(k)
        return pltpu.make_async_remote_copy(
            src_ref=ready.at[c * CH : (c + 1) * CH, other],
            dst_ref=out_ref.at[c * CH : (c + 1) * CH, :, lanes(z)],
            send_sem=zs.at[c, k],
            recv_sem=zr.at[c, k],
            device_id=device,
            device_id_type=MESH,
        )

    def p_copy(c, k):
        other, device = in_plane(k)
        return pltpu.make_async_remote_copy(
            src_ref=in_ref.at[c, other],
            dst_ref=got.at[c, me],
            send_sem=ps.at[c, k],
            recv_sem=pr.at[c, k],
            device_id=device,
            device_id_type=MESH,
        )

    mine = []
    for c in range(NCH):
        each(NS, lambda k: p_copy(c, k).start())
        copy = pltpu.make_async_copy(in_ref.at[c, me], got.at[c, me], own_p.at[c])
        copy.start()
        mine.append(copy)
    last = []
    for c in range(NCH):
        mine[c].wait()
        each(NS, lambda k: p_copy(c, k).wait_recv())
        back = dot(got[c].reshape(NS * 16, NZ * PADR), order_ref[...], 0, 0)
        for i in range(CH):
            block = back[:, i * 128 : (i + 1) * 128].reshape(NZ, PADR, 128)
            ready[c * CH + i] = block[:, :ROWS].astype(BF)
        each(NZ, lambda k: z_copy(c, k).start())
        copy = pltpu.make_async_copy(
            ready.at[c * CH : (c + 1) * CH, z],
            out_ref.at[c * CH : (c + 1) * CH, :, lanes(z)],
            own_z.at[c],
        )
        copy.start()
        last.append(copy)
    for c in range(NCH):
        last[c].wait()
        each(NZ, lambda k: z_copy(c, k).wait())
        each(NS, lambda k: p_copy(c, k).wait_send())


def pair_kernel(
    first_ref, in_ref, panel_ref, target_ref, weight_ref, eig_ref, left_ref, right_ref, rows_ref,
    spectral_ref, out_ref, order, fields, total, mix, spread,
):
    first = first_ref[0, 0]
    tall = NCH * 128
    for b in range(4):
        rows = slice(b * 384, (b + 1) * 384)
        column = lax.broadcasted_iota(jnp.int32, (384, NCOL), 1)
        order[rows, :] = (column == target_ref[rows, :]).astype(F32).astype(BF)
    for j in range(4):
        mix[j * LEV : (j + 1) * LEV, :] = dot(right_ref[...], rows_ref[j]).astype(BF)

    def weigh(t, carry):
        columns = pl.ds(pl.multiple_of(t * 256, 256), 256)
        value = jnp.zeros((tall, 256), F32)
        for b in range(4):
            block = in_ref[:, b * 8 : (b + 1) * 8].reshape(tall, NZ * PADR)
            value += dot(block, order[b * 384 : (b + 1) * 384, columns])
        fields[:, columns] = (value * weight_ref[:, columns]).astype(BF)
        return carry

    lax.fori_loop(0, NCOL // 256, weigh, 0)
    total[...] = jnp.zeros_like(total)

    def solve(t, carry):
        columns = pl.ds(pl.multiple_of(t * 256, 256), 256)
        column = lax.broadcasted_iota(jnp.int32, (1, 256), 1) + t * 256
        owned = column < NCOL - first
        shifted = jnp.where(owned, column, column + first)
        mirror = jnp.where(lax.rem(shifted, 2) == 0, 1.0, -1.0).astype(F32)
        degree = jnp.where(owned, column + first, column).astype(F32)
        factor = degree * (degree + 1.0) / (NCOL * (NCOL - 1.0))
        panel = panel_ref[:, columns]
        even = dot(fields[:, :HALF], panel)
        odd = dot(fields[:, HALF:], panel)
        raw = (even + mirror * odd).astype(BF)
        mixed = dot(mix[...], raw)
        spread_total = jnp.zeros((tall, 256), F32)
        for q in range(2):
            upper = mixed[q * LEV : (q + 1) * LEV]
            lower = mixed[(q + 2) * LEV : (q + 3) * LEV]
            chosen = jnp.where(owned, upper, lower)
            scaled = (chosen / (1.0 + factor * eig_ref[...])).astype(BF)
            solved = dot(left_ref[...], scaled).astype(BF)
            spectral_ref[q, :, columns] = solved
            spread_total += dot(spread[q], solved, 0, 0)
        row = lax.broadcasted_iota(jnp.int32, (tall, 256), 0)
        upper_rows = lax.rem(row, 4) < 2
        kept = jnp.where(upper_rows == owned, spread_total, 0.0)
        total[:, :HALF] += dot(kept.astype(BF), panel, 1, 1)
        total[:, HALF:] += dot((kept * mirror).astype(BF), panel, 1, 1)
        return carry

    for q in range(2):
        spread[q] = (rows_ref[q].astype(F32) + rows_ref[q + 2].astype(F32)).astype(BF)
    lax.fori_loop(0, NCOL // 256, solve, 0)
    fields[...] = total[...].astype(BF)
    for b in range(4):
        value = dot(fields[...], order[b * 384 : (b + 1) * 384, :], 1, 1).astype(BF)
        out_ref[:, b * 8 : (b + 1) * 8] = value.reshape(NCH, 8, 16, NZ * PADR)


def exchange_scratch():
    return [
        pltpu.SemaphoreType.DMA((NCH, NZ)),
        pltpu.SemaphoreType.DMA((NCH, NZ)),
        pltpu.SemaphoreType.DMA((NCH, NS)),
        pltpu.SemaphoreType.DMA((NCH, NS)),
        pltpu.SemaphoreType.DMA((NCH,)),
        pltpu.SemaphoreType.DMA((NCH,)),
    ]


def body(state, panels, pair_table, lat_order, gauss_weights, eig, left, right):
    table = jnp.asarray(dft_table())
    order = jnp.asarray(lane_order())
    rows = jnp.asarray(level_rows())
    wave = jnp.stack([pair_table, NCOL - pair_table], axis=1).reshape(1, -1)
    pos = (wave % 2) * HALF + wave // 2
    by_plane = jnp.transpose(lat_order.reshape(NZ, 4, ROWS), (1, 0, 2))
    target = jnp.where(by_plane < HALF, by_plane, HALF + 2 * HALF - 1 - by_plane)
    target = jnp.pad(target, ((0, 0), (0, 0), (0, PADR - ROWS)), constant_values=-1).reshape(-1, 1)
    weights = jnp.concatenate([gauss_weights[:HALF], gauss_weights[HALF:][::-1]]).reshape(1, -1)
    owner = lax.axis_index("wave") * 8 + lax.axis_index("lev")
    first = lax.dynamic_slice(pair_table, (owner,), (1,)).reshape(1, 1)
    flat = LEVD * PADR
    plain = pltpu.CompilerParams(vmem_limit_bytes=LIMIT)
    sent = pl.pallas_call(
        fourier_kernel,
        out_shape=jax.ShapeDtypeStruct((LEVD, ROWS, NZ * 128), BF),
        in_specs=[VM] * 3,
        out_specs=VM,
        scratch_shapes=[pltpu.VMEM((LEVD, PADR, NLON), F32), pltpu.VMEM((2 * flat, NCOL), BF)],
        compiler_params=plain,
        name="fourier",
    )(state, table, pos)
    wire = (NCH, NS, 16, NZ * PADR)
    arrived = pl.pallas_call(
        to_pairs_kernel,
        out_shape=jax.ShapeDtypeStruct(wire, BF),
        in_specs=[VM] * 2,
        out_specs=VM,
        scratch_shapes=[
            pltpu.VMEM((LEVD, NZ, ROWS, 128), BF),
            pltpu.VMEM(wire, BF),
            pltpu.VMEM((CH, NZ, PADR, 128), F32),
            *exchange_scratch(),
        ],
        compiler_params=pltpu.CompilerParams(
            collective_id=0, has_side_effects=True, vmem_limit_bytes=LIMIT
        ),
        name="to_pairs",
    )(sent, order)
    spectral, back = pl.pallas_call(
        pair_kernel,
        out_shape=(
            jax.ShapeDtypeStruct((2, LEV, NCOL), BF),
            jax.ShapeDtypeStruct(wire, BF),
        ),
        in_specs=[SM] + [VM] * 8,
        out_specs=(VM, VM),
        scratch_shapes=[
            pltpu.VMEM((4 * NZ * PADR, NCOL), BF),
            pltpu.VMEM((NCH * 128, NCOL), BF),
            pltpu.VMEM((NCH * 128, NCOL), F32),
            pltpu.VMEM((4 * LEV, NCH * 128), BF),
            pltpu.VMEM((2, LEV, NCH * 128), BF),
        ],
        compiler_params=plain,
        name="pair",
    )(first, arrived, panels[0], target, weights, eig.reshape(-1, 1), left, right, rows)
    returned = pl.pallas_call(
        to_rows_kernel,
        out_shape=jax.ShapeDtypeStruct((LEVD, ROWS, NZ * 128), BF),
        in_specs=[VM] * 2,
        out_specs=VM,
        scratch_shapes=[
            pltpu.VMEM(wire, BF),
            pltpu.VMEM((LEVD, NZ, ROWS, 128), BF),
            *exchange_scratch(),
        ],
        compiler_params=pltpu.CompilerParams(
            collective_id=1, has_side_effects=True, vmem_limit_bytes=LIMIT
        ),
        name="to_rows",
    )(back, order)
    new_state = pl.pallas_call(
        inverse_kernel,
        out_shape=jax.ShapeDtypeStruct((LEVD, ROWS, NLON), BF),
        in_specs=[VM] * 3,
        out_specs=VM,
        scratch_shapes=[
            pltpu.VMEM((LEVD, PADR, NZ * 128), F32),
            pltpu.VMEM((2 * flat, NZ * 64), BF),
            pltpu.VMEM((2, flat, NCOL), BF),
        ],
        compiler_params=plain,
        name="inverse",
    )(returned, table, pos)
    return new_state, spectral[None]


def solution(mesh):
    return jax.shard_map(
        body,
        mesh=mesh,
        in_specs=(
            P("lev", "wave", None),
            P(("wave", "lev"), None, None),
            P(),
            P(),
            P(),
            P(),
            P(),
            P(),
        ),
        out_specs=(P("lev", "wave", None), P(("wave", "lev"), None, None, None)),
        check_vma=False,
    )
```

```python
import math

import jax
import jax.numpy as jnp
import ml_dtypes
import numpy as np
from jax import lax
from jax.experimental import pallas as pl
from jax.experimental.pallas import tpu as pltpu
from jax.sharding import PartitionSpec as P

NLON = 2560
NCOL = 1280
HALF = 640
LEV = 72
LEVD = 9
ROWS = 20
PADR = 24
NZ = 16
NS = 32
CH = 3
NCH = LEVD // CH
MESH = pl.DeviceIdType.MESH
VM = pl.BlockSpec(memory_space=pltpu.VMEM)
SM = pl.BlockSpec(memory_space=pltpu.SMEM)
F32 = jnp.float32
BF = jnp.bfloat16
LIMIT = 56 * 1024 * 1024


def dft_table():
    x = np.arange(NLON // 2, dtype=np.int64)
    out = []
    for parity in (0, 1):
        m = 2 * np.arange(HALF, dtype=np.int64) + parity
        angle = (x[:, None] * m[None, :] % NLON) * (2.0 * math.pi / NLON)
        both = np.concatenate([np.cos(angle), -np.sin(angle)], axis=1)
        out.append(both * (1.0 / math.sqrt(NLON)))
    return np.stack(out).astype(np.float32).astype(ml_dtypes.bfloat16)


def lane_order():
    e = np.zeros((NS, 16, CH, 2, 2, NS), np.float32)
    for d in range(NS):
        for i in range(CH):
            for ab in range(2):
                for q in range(2):
                    e[d, i * 4 + ab * 2 + q, i, ab, q, d] = 1.0
    return e.reshape(NS * 16, CH * 128).astype(ml_dtypes.bfloat16)


def level_rows():
    o = np.zeros((4, LEV, NCH, 8, 16), np.float32)
    for c in range(NCH):
        for g in range(8):
            for i in range(CH):
                for j in range(4):
                    o[j, g * LEVD + c * CH + i, c, g, i * 4 + j] = 1.0
    return o.reshape(4, LEV, NCH * 128).astype(ml_dtypes.bfloat16)


def dot(a, b, ca=1, cb=0):
    return lax.dot_general(a, b, (((ca,), (cb,)), ((), ())), preferred_element_type=F32)


def each(count, act):
    def one(k, carry):
        act(k)
        return carry

    lax.fori_loop(1, count, one, 0)


def lanes(z):
    return pl.ds(pl.multiple_of(z * 128, 128), 128)


def iota(shape, axis):
    return lax.broadcasted_iota(jnp.int32, shape, axis)


def step_kernel(
    table_pairs, state_hbm, panel_hbm, table_hbm, pairs_ref, target_ref, weight_ref, eig_ref, left_ref, right_ref,
    lane_ref, rows_ref, new_ref, spectral_ref,
    state, panel, table, pick, order, grid, spec, sent, got_z, wide, made, got_p, tall, raw, mix, spread, solved,
    part, home, got_q, ready_z, returned, chosen, waves,
    load, zs, zr, ps, pr, own, qs, qr, ys, yr,
):
    wave, group = lax.axis_index("wave"), lax.axis_index("lev")
    z, s = wave // 4, lax.rem(wave, 4)
    me = s * 8 + group
    first = table_pairs[wave * 8 + group]
    flat = CH * PADR

    def along_z(k):
        step = (k + 0) // 2
        other = lax.rem(z + 8 + step * (1 - 2 * lax.rem(k, 2)) + NZ, NZ)
        return other, (other * 4 + s, group)

    def in_plane(k):
        other = lax.rem(me + k, NS)
        return other, (z * 4 + other // 8, lax.rem(other, 8))

    barrier = pltpu.get_barrier_semaphore()

    def hail(of):
        def act(k):
            pl.semaphore_signal(barrier, inc=1, device_id=of(k)[1], device_id_type=MESH)

        return act

    each(NZ, hail(along_z))
    each(NS, hail(in_plane))

    loads = [pltpu.make_async_copy(table_hbm.at[p], table.at[p], load.at[p]) for p in range(2)]
    for c in range(NCH):
        part_of = slice(c * CH, (c + 1) * CH)
        loads.append(pltpu.make_async_copy(state_hbm.at[part_of], state.at[part_of], load.at[2 + c]))
    loads.append(pltpu.make_async_copy(panel_hbm.at[0], panel, load.at[2 + NCH]))
    for n in (2, 0, 1, 3, 4, 5):
        loads[n].start()

    def remote(src, dst, send, recv, device):
        return pltpu.make_async_remote_copy(
            src_ref=src, dst_ref=dst, send_sem=send, recv_sem=recv, device_id=device, device_id_type=MESH
        )

    def levels(c):
        return slice(c * CH, (c + 1) * CH)

    def z_out(c, k):
        other, device = along_z(k)
        return remote(sent.at[levels(c), :, lanes(other)], got_z.at[levels(c), z], zs.at[c, k], zr.at[c, k], device)

    def p_out(c, k):
        other, device = in_plane(k)
        return remote(made.at[c, other], got_p.at[c, me], ps.at[c, k], pr.at[c, k], device)

    def p_back(c, k):
        other, device = in_plane(k)
        return remote(home.at[c, other], got_q.at[c, me], qs.at[c, k], qr.at[c, k], device)

    def z_back(c, k):
        other, device = along_z(k)
        return remote(ready_z.at[levels(c), other], returned.at[levels(c), :, lanes(z)], ys.at[c, k], yr.at[c, k], device)

    lane = iota((8, 128), 1)
    for t in range(NZ // 2):
        here = jnp.broadcast_to(pairs_ref[t // 2 : t // 2 + 1, :], (8, 128))
        there = pltpu.roll(here, 64, 1)
        low, high = (here, there) if t % 2 == 0 else (there, here)
        number = jnp.where(lane < 64, low, NCOL - high)
        pos = (lax.rem(number, 2) * HALF + lax.shift_right_logical(number, 1))[:1]
        pick[:, t * 128 : (t + 1) * 128] = (iota((NCOL, 128), 0) == pos).astype(F32).astype(BF)
    grid[...] = jnp.zeros_like(grid)
    wide[...] = jnp.zeros_like(wide)
    tall[...] = jnp.zeros_like(tall)
    chosen[...] = jnp.zeros_like(chosen)
    even_group = lax.rem(iota((flat, 128), 1) // 32, 2) == 0

    mine = []
    for c in range(NCH):
        loads[2 + c].wait()
        grid[:, :ROWS, :] = state[levels(c)].astype(F32)
        low = grid[:, :, : NLON // 2].reshape(flat, NLON // 2)
        high = grid[:, :, NLON // 2 :].reshape(flat, NLON // 2)
        for parity, half in ((0, low + high), (1, low - high)):
            if c == 0:
                loads[parity].wait()
            both = dot(half.astype(BF), table[parity]).astype(BF)
            spec[:flat, parity * HALF : (parity + 1) * HALF] = both[:, :HALF]
            spec[flat:, parity * HALF : (parity + 1) * HALF] = both[:, HALF:]
        for t in range(NZ // 2):
            got = dot(spec[...], pick[:, t * 128 : (t + 1) * 128])
            cos, sin = got[:flat], got[flat:]
            one = jnp.where(even_group, cos, pltpu.roll(sin, 32, 1))
            two = jnp.where(even_group, pltpu.roll(cos, 96, 1), sin)
            for h, value in ((0, one), (1, two)):
                columns = slice((2 * t + h) * 128, (2 * t + h + 1) * 128)
                sent[levels(c), :, columns] = value.reshape(CH, PADR, 128)[:, :ROWS].astype(BF)
        if c == 0:
            pl.semaphore_wait(barrier, NZ - 1 + NS - 1)
        each(NZ, lambda k: z_out(c, k).start())
        copy = pltpu.make_async_copy(sent.at[levels(c), :, lanes(z)], got_z.at[levels(c), z], own.at[c])
        copy.start()
        mine.append(copy)

    def build(t, carry):
        rows = pl.ds(pl.multiple_of(t * 128, 128), 128)
        order[rows, :] = (iota((128, 4 * NZ * PADR), 0) + t * 128 == target_ref[...]).astype(F32).astype(BF)
        return carry

    lax.fori_loop(0, NCOL // 128, build, 0)
    for j in range(4):
        mix[j * LEV : (j + 1) * LEV, :] = dot(right_ref[...], rows_ref[j]).astype(BF)
    for q in range(2):
        spread[q] = (rows_ref[q].astype(F32) + rows_ref[q + 2].astype(F32)).astype(BF)
    eig = jnp.sum(
        jnp.where(iota((LEV, LEV), 0) == iota((LEV, LEV), 1), eig_ref[...], 0.0), axis=1, keepdims=True
    )

    def column_facts(start, width):
        column = iota((1, width), 1) + start
        owned = column < NCOL - first
        shifted = jnp.where(owned, column, column + first)
        mirror = jnp.where(lax.rem(shifted, 2) == 0, 1.0, -1.0).astype(F32)
        return column, owned, mirror

    def turn(c):
        mine[c].wait()
        each(NZ, lambda k: z_out(c, k).wait_recv())
        for i in range(CH):
            wide[i, :, :ROWS, :] = got_z[c * CH + i].astype(F32)
        block = jnp.concatenate(
            [wide[i].reshape(NZ * PADR, 128).astype(BF) for i in range(CH)], axis=1
        )
        value = dot(lane_ref[...], block, 1, 1).reshape(NS, 16, NZ * PADR)
        made[c] = value[:, : 4 * CH].astype(BF)
        each(NS, lambda k: p_out(c, k).start())
        copy = pltpu.make_async_copy(made.at[c, me], got_p.at[c, me], own.at[NCH + c])
        copy.start()
        return copy

    def legendre(c, copy):
        copy.wait()
        each(NS, lambda k: p_out(c, k).wait_recv())
        tall[:, : 4 * CH, :] = got_p[c].astype(F32)
        block = jnp.concatenate(
            [tall[b * 8 : (b + 1) * 8].reshape(128, NZ * PADR).astype(BF) for b in range(4)], axis=1
        )
        value = dot(block, order[...], 1, 1)
        part[...] = (value * weight_ref[...]).astype(BF)
        mirror = column_facts(0, NCOL)[2]
        even = dot(part[:, :HALF], panel[...])
        odd = dot(part[:, HALF:], panel[...])
        raw[c * 128 : (c + 1) * 128, :] = (even + mirror * odd).astype(BF)

    copies = [turn(0), turn(1)]
    loads[2 + NCH].wait()
    legendre(0, copies[0])
    copies.append(turn(2))
    legendre(1, copies[1])
    legendre(2, copies[2])

    def solve(t, carry):
        columns = pl.ds(pl.multiple_of(t * 256, 256), 256)
        column, owned, _ = column_facts(t * 256, 256)
        degree = jnp.where(owned, column + first, column).astype(F32)
        factor = degree * (degree + 1.0) / (NCOL * (NCOL - 1.0))
        mixed = dot(mix[...], raw[:, columns])
        for q in range(2):
            upper = mixed[q * LEV : (q + 1) * LEV]
            lower = mixed[(q + 2) * LEV : (q + 3) * LEV]
            scaled = (jnp.where(owned, upper, lower) / (1.0 + factor * eig)).astype(BF)
            value = dot(left_ref[...], scaled).astype(BF)
            solved[q, :, columns] = value
            spectral_ref[q, :, columns] = value
        return carry

    lax.fori_loop(0, NCOL // 256, solve, 0)

    homes = []
    for c in range(NCH):
        _, owned, mirror = column_facts(0, NCOL)
        value = dot(spread[0, :, c * 128 : (c + 1) * 128], solved[0], 0, 0)
        value += dot(spread[1, :, c * 128 : (c + 1) * 128], solved[1], 0, 0)
        kept = jnp.where((lax.rem(iota((128, NCOL), 0), 4) < 2) == owned, value, 0.0)
        part[:, :HALF] = dot(kept.astype(BF), panel[...], 1, 1).astype(BF)
        part[:, HALF:] = dot((kept * mirror).astype(BF), panel[...], 1, 1).astype(BF)
        for b in range(4):
            value = dot(part[...], order[:, b * 384 : (b + 1) * 384])
            home[c, b * 8 : (b + 1) * 8] = value.reshape(8, 16, NZ * PADR)[:, : 4 * CH].astype(BF)
        each(NS, lambda k: p_back(c, k).start())
        copy = pltpu.make_async_copy(home.at[c, me], got_q.at[c, me], own.at[2 * NCH + c])
        copy.start()
        homes.append(copy)
    lasts = []
    for c in range(NCH):
        homes[c].wait()
        each(NS, lambda k: p_back(c, k).wait_recv())
        tall[:, : 4 * CH, :] = got_q[c].astype(F32)
        value = dot(tall[...].reshape(NS * 16, NZ * PADR).astype(BF), lane_ref[...], 0, 0)
        for i in range(CH):
            block = value[:, i * 128 : (i + 1) * 128].reshape(NZ, PADR, 128)
            ready_z[c * CH + i] = block[:, :ROWS].astype(BF)
        each(NZ, lambda k: z_back(c, k).start())
        copy = pltpu.make_async_copy(ready_z.at[levels(c), z], returned.at[levels(c), :, lanes(z)], own.at[3 * NCH + c])
        copy.start()
        lasts.append(copy)
    for c in range(NCH):
        each(NZ, lambda k: z_out(c, k).wait_send())
        each(NS, lambda k: p_out(c, k).wait_send())
        each(NS, lambda k: p_back(c, k).wait_send())

    for c in range(NCH):
        lasts[c].wait()
        each(NZ, lambda k: z_back(c, k).wait_recv())
        chosen[:, :ROWS, :] = returned[levels(c)].astype(F32)
        for t in range(NZ // 2):
            one = chosen[:, :, 2 * t * 128 : (2 * t + 1) * 128].reshape(flat, 128)
            two = chosen[:, :, (2 * t + 1) * 128 : (2 * t + 2) * 128].reshape(flat, 128)
            columns = slice(t * 128, (t + 1) * 128)
            waves[:flat, columns] = jnp.where(even_group, one, pltpu.roll(two, 32, 1)).astype(BF)
            waves[flat:, columns] = jnp.where(even_group, pltpu.roll(one, 96, 1), two).astype(BF)
        both = dot(waves[...], pick[...], 1, 1).astype(BF)
        for t in range(NLON // 2 // 256):
            rows = slice(t * 256, (t + 1) * 256)
            sums = []
            for parity in range(2):
                numbers = slice(parity * HALF, (parity + 1) * HALF)
                sums.append(
                    dot(both[:flat, numbers], table[parity, rows, :HALF], 1, 1)
                    + dot(both[flat:, numbers], table[parity, rows, HALF:], 1, 1)
                )
            low = (2.0 * (sums[0] + sums[1])).reshape(CH, PADR, 256)
            high = (2.0 * (sums[0] - sums[1])).reshape(CH, PADR, 256)
            new_ref[levels(c), :, rows] = low[:, :ROWS].astype(BF)
            new_ref[levels(c), :, NLON // 2 + t * 256 : NLON // 2 + (t + 1) * 256] = high[:, :ROWS].astype(BF)
    for c in range(NCH):
        each(NZ, lambda k: z_back(c, k).wait_send())


def body(state, panels, pair_table, lat_order, gauss_weights, eig, left, right):
    by_plane = jnp.transpose(lat_order.reshape(NZ, 4, ROWS), (1, 0, 2))
    target = jnp.where(by_plane < HALF, by_plane, HALF + 2 * HALF - 1 - by_plane)
    target = jnp.pad(target, ((0, 0), (0, 0), (0, PADR - ROWS)), constant_values=-1).reshape(1, -1)
    weights = jnp.concatenate([gauss_weights[:HALF], gauss_weights[HALF:][::-1]]).reshape(1, -1)
    flat = CH * PADR
    wire = (NCH, NS, 4 * CH, NZ * PADR)
    along = (LEVD, NZ, ROWS, 128)
    z_sems, p_sems = pltpu.SemaphoreType.DMA((NCH, NZ)), pltpu.SemaphoreType.DMA((NCH, NS))
    new_state, spectral = pl.pallas_call(
        step_kernel,
        out_shape=(
            jax.ShapeDtypeStruct((LEVD, ROWS, NLON), BF),
            jax.ShapeDtypeStruct((2, LEV, NCOL), BF),
        ),
        in_specs=[SM] + [pl.BlockSpec(memory_space=pl.ANY)] * 3 + [VM] * 8,
        out_specs=(VM, VM),
        scratch_shapes=[
            pltpu.VMEM((LEVD, ROWS, NLON), BF),
            pltpu.VMEM((HALF, NCOL), BF),
            pltpu.VMEM((2, NCOL, NCOL), BF),
            pltpu.VMEM((NCOL, NZ * 64), BF),
            pltpu.VMEM((NCOL, 4 * NZ * PADR), BF),
            pltpu.VMEM((CH, PADR, NLON), F32),
            pltpu.VMEM((2 * flat, NCOL), BF),
            pltpu.VMEM((LEVD, ROWS, NZ * 128), BF),
            pltpu.VMEM(along, BF),
            pltpu.VMEM((CH, NZ, PADR, 128), F32),
            pltpu.VMEM(wire, BF),
            pltpu.VMEM(wire, BF),
            pltpu.VMEM((NS, 16, NZ * PADR), F32),
            pltpu.VMEM((NCH * 128, NCOL), BF),
            pltpu.VMEM((4 * LEV, NCH * 128), BF),
            pltpu.VMEM((2, LEV, NCH * 128), BF),
            pltpu.VMEM((2, LEV, NCOL), BF),
            pltpu.VMEM((128, NCOL), BF),
            pltpu.VMEM(wire, BF),
            pltpu.VMEM(wire, BF),
            pltpu.VMEM(along, BF),
            pltpu.VMEM((LEVD, ROWS, NZ * 128), BF),
            pltpu.VMEM((CH, PADR, NZ * 128), F32),
            pltpu.VMEM((2 * flat, NZ * 64), BF),
            pltpu.SemaphoreType.DMA((3 + NCH,)),
            z_sems, z_sems, p_sems, p_sems,
            pltpu.SemaphoreType.DMA((4 * NCH,)),
            p_sems, p_sems, z_sems, z_sems,
        ],
        compiler_params=pltpu.CompilerParams(
            collective_id=0, has_side_effects=True, vmem_limit_bytes=LIMIT
        ),
        name="step",
    )(
        pair_table, state, panels, jnp.asarray(dft_table()), pair_table.reshape(4, 128), target, weights,
        eig.reshape(1, -1), left, right, jnp.asarray(lane_order()), jnp.asarray(level_rows()),
    )
    return new_state, spectral[None]


def solution(mesh):
    return jax.shard_map(
        body,
        mesh=mesh,
        in_specs=(
            P("lev", "wave", None),
            P(("wave", "lev"), None, None),
            P(),
            P(),
            P(),
            P(),
            P(),
            P(),
        ),
        out_specs=(P("lev", "wave", None), P(("wave", "lev"), None, None, None)),
        check_vma=False,
    )
```

```python
import math

import jax
import jax.numpy as jnp
import ml_dtypes
import numpy as np
from jax import lax
from jax.experimental import pallas as pl
from jax.experimental.pallas import tpu as pltpu
from jax.sharding import PartitionSpec as P

NLON = 2560
NCOL = 1280
HALF = 640
LEV = 72
LEVD = 9
ROWS = 20
PADR = 24
NZ = 16
NS = 32
CH = 3
NCH = LEVD // CH
MESH = pl.DeviceIdType.MESH
VM = pl.BlockSpec(memory_space=pltpu.VMEM)
SM = pl.BlockSpec(memory_space=pltpu.SMEM)
F32 = jnp.float32
BF = jnp.bfloat16
LIMIT = 56 * 1024 * 1024


def dft_table():
    x = np.arange(NLON // 2, dtype=np.int64)
    out = []
    for parity in (0, 1):
        m = 2 * np.arange(HALF, dtype=np.int64) + parity
        angle = (x[:, None] * m[None, :] % NLON) * (2.0 * math.pi / NLON)
        both = np.concatenate([np.cos(angle), -np.sin(angle)], axis=1)
        out.append(both * (1.0 / math.sqrt(NLON)))
    return np.stack(out).astype(np.float32).astype(ml_dtypes.bfloat16)


def lane_order():
    e = np.zeros((NS, 16, CH, 2, 2, NS), np.float32)
    for d in range(NS):
        for i in range(CH):
            for ab in range(2):
                for q in range(2):
                    e[d, i * 4 + ab * 2 + q, i, ab, q, d] = 1.0
    return e.reshape(NS * 16, CH * 128).astype(ml_dtypes.bfloat16)


def level_rows():
    o = np.zeros((4, LEV, NCH, 8, 16), np.float32)
    for c in range(NCH):
        for g in range(8):
            for i in range(CH):
                for j in range(4):
                    o[j, g * LEVD + c * CH + i, c, g, i * 4 + j] = 1.0
    return o.reshape(4, LEV, NCH * 128).astype(ml_dtypes.bfloat16)


def dot(a, b, ca=1, cb=0):
    return lax.dot_general(a, b, (((ca,), (cb,)), ((), ())), preferred_element_type=F32)


def each(count, act):
    def one(k, carry):
        act(k)
        return carry

    lax.fori_loop(1, count, one, 0)


def lanes(z):
    return pl.ds(pl.multiple_of(z * 128, 128), 128)


def iota(shape, axis):
    return lax.broadcasted_iota(jnp.int32, shape, axis)


def step_kernel(
    table_pairs, state_hbm, panel_hbm, table_hbm, pairs_ref, target_ref, weight_ref, eig_ref, left_ref, right_ref,
    lane_ref, rows_ref, new_ref, spectral_ref,
    state, panel, table, pick, order, grid, spec, sent, got_z, wide, made, got_p, tall, raw, mix, spread, solved,
    part, masked, scale, home, got_q, ready_z, returned, chosen, waves,
    load, zs, zr, ps, pr, own, qs, qr, ys, yr,
):
    wave, group = lax.axis_index("wave"), lax.axis_index("lev")
    z, s = wave // 4, lax.rem(wave, 4)
    me = s * 8 + group
    first = table_pairs[wave * 8 + group]
    flat = CH * PADR

    def along_z(k):
        step = (k + 0) // 2
        other = lax.rem(z + 8 + step * (1 - 2 * lax.rem(k, 2)) + NZ, NZ)
        return other, (other * 4 + s, group)

    def in_plane(k):
        other = lax.rem(me + k, NS)
        return other, (z * 4 + other // 8, lax.rem(other, 8))

    loads = [pltpu.make_async_copy(table_hbm.at[p], table.at[p], load.at[p]) for p in range(2)]
    for c in range(NCH):
        part_of = slice(c * CH, (c + 1) * CH)
        loads.append(pltpu.make_async_copy(state_hbm.at[part_of], state.at[part_of], load.at[2 + c]))
    loads.append(pltpu.make_async_copy(panel_hbm.at[0], panel, load.at[2 + NCH]))
    for n in (2, 0, 1, 3, 4, 5):
        loads[n].start()

    barrier = pltpu.get_barrier_semaphore()

    def hail(of):
        def act(k):
            pl.semaphore_signal(barrier, inc=1, device_id=of(k)[1], device_id_type=MESH)

        return act

    each(NZ, hail(along_z))
    each(NS, hail(in_plane))

    def remote(src, dst, send, recv, device):
        return pltpu.make_async_remote_copy(
            src_ref=src, dst_ref=dst, send_sem=send, recv_sem=recv, device_id=device, device_id_type=MESH
        )

    def levels(c):
        return slice(c * CH, (c + 1) * CH)

    def z_out(c, k):
        other, device = along_z(k)
        return remote(sent.at[levels(c), :, lanes(other)], got_z.at[levels(c), z], zs.at[c], zr.at[c], device)

    def p_out(c, k):
        other, device = in_plane(k)
        return remote(made.at[c, other], got_p.at[c, me], ps.at[c], pr.at[c], device)

    def p_back(c, k):
        other, device = in_plane(k)
        return remote(home.at[c, other], got_q.at[c, me], qs.at[c], qr.at[c], device)

    def z_back(c, k):
        other, device = along_z(k)
        return remote(ready_z.at[levels(c), other], returned.at[levels(c), :, lanes(z)], ys.at[c], yr.at[c], device)

    def whole(ref, send, recv, device):
        return remote(ref, ref, send, recv, device)

    def all_z_out(c):
        return whole(got_z.at[levels(c), : NZ - 1], zs.at[c], zr.at[c], along_z(1)[1])

    def all_p_out(c):
        return whole(got_p.at[c, : NS - 1], ps.at[c], pr.at[c], in_plane(1)[1])

    def all_p_back(c):
        return whole(got_q.at[c, : NS - 1], qs.at[c], qr.at[c], in_plane(1)[1])

    def all_z_back(c):
        return whole(ready_z.at[levels(c), : NZ - 1], ys.at[c], yr.at[c], along_z(1)[1])

    lane = iota((8, 128), 1)
    for t in range(NZ // 2):
        here = jnp.broadcast_to(pairs_ref[t // 2 : t // 2 + 1, :], (8, 128))
        there = pltpu.roll(here, 64, 1)
        low, high = (here, there) if t % 2 == 0 else (there, here)
        number = jnp.where(lane < 64, low, NCOL - high)
        pos = (lax.rem(number, 2) * HALF + lax.shift_right_logical(number, 1))[:1]
        pick[:, t * 128 : (t + 1) * 128] = (iota((NCOL, 128), 0) == pos).astype(F32).astype(BF)
    grid[...] = jnp.zeros_like(grid)
    wide[...] = jnp.zeros_like(wide)
    tall[...] = jnp.zeros_like(tall)
    chosen[...] = jnp.zeros_like(chosen)
    even_group = lax.rem(iota((flat, 128), 1) // 32, 2) == 0

    mine = []
    for c in range(NCH):
        loads[2 + c].wait()
        grid[:, :ROWS, :] = state[levels(c)].astype(F32)
        low = grid[:, :, : NLON // 2].reshape(flat, NLON // 2)
        high = grid[:, :, NLON // 2 :].reshape(flat, NLON // 2)
        for parity, half in ((0, low + high), (1, low - high)):
            if c == 0:
                loads[parity].wait()
            both = dot(half.astype(BF), table[parity]).astype(BF)
            spec[:flat, parity * HALF : (parity + 1) * HALF] = both[:, :HALF]
            spec[flat:, parity * HALF : (parity + 1) * HALF] = both[:, HALF:]
        for t in range(NZ // 2):
            got = dot(spec[...], pick[:, t * 128 : (t + 1) * 128])
            cos, sin = got[:flat], got[flat:]
            one = jnp.where(even_group, cos, pltpu.roll(sin, 32, 1))
            two = jnp.where(even_group, pltpu.roll(cos, 96, 1), sin)
            for h, value in ((0, one), (1, two)):
                columns = slice((2 * t + h) * 128, (2 * t + h + 1) * 128)
                sent[levels(c), :, columns] = value.reshape(CH, PADR, 128)[:, :ROWS].astype(BF)
        if c == 0:
            pl.semaphore_wait(barrier, NZ - 1 + NS - 1)
        each(NZ, lambda k: z_out(c, k).start())
        copy = pltpu.make_async_copy(sent.at[levels(c), :, lanes(z)], got_z.at[levels(c), z], own.at[c])
        copy.start()
        mine.append(copy)

    def build(t, carry):
        rows = pl.ds(pl.multiple_of(t * 128, 128), 128)
        order[rows, :] = (iota((128, 4 * NZ * PADR), 0) + t * 128 == target_ref[...]).astype(F32).astype(BF)
        return carry

    lax.fori_loop(0, NCOL // 128, build, 0)
    for j in range(4):
        mix[j * LEV : (j + 1) * LEV, :] = dot(right_ref[...], rows_ref[j]).astype(BF)
    for q in range(2):
        spread[q] = (rows_ref[q].astype(F32) + rows_ref[q + 2].astype(F32)).astype(BF)
    eig = jnp.sum(
        jnp.where(iota((LEV, LEV), 0) == iota((LEV, LEV), 1), eig_ref[...], 0.0), axis=1, keepdims=True
    )

    row, column = iota((HALF, HALF), 0), iota((HALF, HALF), 1)
    south = jnp.where(row + column == HALF - 1, weight_ref[:, HALF:], 0.0)
    south = jnp.where(row == column, jnp.sum(south, axis=1, keepdims=True), 0.0)
    scale[:, :HALF] = weight_ref[:, :HALF]
    scale[:, HALF:] = jnp.sum(south, axis=0, keepdims=True)

    def column_facts(start, width):
        column = iota((1, width), 1) + start
        owned = column < NCOL - first
        shifted = jnp.where(owned, column, column + first)
        mirror = jnp.where(lax.rem(shifted, 2) == 0, 1.0, -1.0).astype(F32)
        return column, owned, mirror

    def turn(c):
        mine[c].wait()
        all_z_out(c).wait_recv()
        for i in range(CH):
            wide[i, :, :ROWS, :] = got_z[c * CH + i].astype(F32)
        block = jnp.concatenate(
            [wide[i].reshape(NZ * PADR, 128).astype(BF) for i in range(CH)], axis=1
        )
        value = dot(lane_ref[...], block, 1, 1).reshape(NS, 16, NZ * PADR)
        made[c] = value[:, : 4 * CH].astype(BF)
        each(NS, lambda k: p_out(c, k).start())
        copy = pltpu.make_async_copy(made.at[c, me], got_p.at[c, me], own.at[NCH + c])
        copy.start()
        return copy

    def legendre(c, copy):
        copy.wait()
        all_p_out(c).wait_recv()
        tall[:, : 4 * CH, :] = got_p[c].astype(F32)
        block = jnp.concatenate(
            [tall[b * 8 : (b + 1) * 8].reshape(128, NZ * PADR).astype(BF) for b in range(4)], axis=1
        )
        value = dot(block, order[...], 1, 1)
        weighted = (value * scale[...]).astype(BF)
        part[:128] = weighted[:, :HALF]
        part[128:] = weighted[:, HALF:]
        mirror = column_facts(0, NCOL)[2]
        both = dot(part[...], panel[...])
        raw[c * 128 : (c + 1) * 128, :] = (both[:128] + mirror * both[128:]).astype(BF)

    copies = [turn(0), turn(1)]
    loads[2 + NCH].wait()
    legendre(0, copies[0])
    copies.append(turn(2))
    legendre(1, copies[1])
    legendre(2, copies[2])

    def solve(t, carry):
        columns = pl.ds(pl.multiple_of(t * 256, 256), 256)
        column, owned, _ = column_facts(t * 256, 256)
        degree = jnp.where(owned, column + first, column).astype(F32)
        factor = degree * (degree + 1.0) / (NCOL * (NCOL - 1.0))
        mixed = dot(mix[...], raw[:, columns])
        for q in range(2):
            upper = mixed[q * LEV : (q + 1) * LEV]
            lower = mixed[(q + 2) * LEV : (q + 3) * LEV]
            scaled = (jnp.where(owned, upper, lower) / (1.0 + factor * eig)).astype(BF)
            value = dot(left_ref[...], scaled).astype(BF)
            solved[q, :, columns] = value
            spectral_ref[q, :, columns] = value
        return carry

    lax.fori_loop(0, NCOL // 256, solve, 0)

    def leave(c):
        _, owned, mirror = column_facts(0, NCOL)
        value = dot(spread[0, :, c * 128 : (c + 1) * 128], solved[0], 0, 0)
        value += dot(spread[1, :, c * 128 : (c + 1) * 128], solved[1], 0, 0)
        kept = jnp.where((lax.rem(iota((128, NCOL), 0), 4) < 2) == owned, value, 0.0)
        masked[:128] = kept.astype(BF)
        masked[128:] = (kept * mirror).astype(BF)
        both = dot(masked[...], panel[...], 1, 1).astype(BF)
        by_lat = jnp.concatenate([both[:128], both[128:]], axis=1)
        for b in range(4):
            value = dot(by_lat, order[:, b * 384 : (b + 1) * 384])
            home[c, b * 8 : (b + 1) * 8] = value.reshape(8, 16, NZ * PADR)[:, : 4 * CH].astype(BF)
        each(NS, lambda k: p_back(c, k).start())
        copy = pltpu.make_async_copy(home.at[c, me], got_q.at[c, me], own.at[2 * NCH + c])
        copy.start()
        return copy

    def retrace(c, arrived):
        arrived.wait()
        all_p_back(c).wait_recv()
        tall[:, : 4 * CH, :] = got_q[c].astype(F32)
        value = dot(tall[...].reshape(NS * 16, NZ * PADR).astype(BF), lane_ref[...], 0, 0)
        for i in range(CH):
            block = value[:, i * 128 : (i + 1) * 128].reshape(NZ, PADR, 128)
            ready_z[c * CH + i] = block[:, :ROWS].astype(BF)
        each(NZ, lambda k: z_back(c, k).start())
        copy = pltpu.make_async_copy(ready_z.at[levels(c), z], returned.at[levels(c), :, lanes(z)], own.at[3 * NCH + c])
        copy.start()
        return copy

    homes = [leave(0), leave(1)]
    lasts = [retrace(0, homes[0])]
    homes.append(leave(2))
    lasts += [retrace(1, homes[1]), retrace(2, homes[2])]
    for c in range(NCH):
        all_z_out(c).wait_send()
        all_p_out(c).wait_send()
        all_p_back(c).wait_send()

    for c in range(NCH):
        lasts[c].wait()
        all_z_back(c).wait_recv()
        chosen[:, :ROWS, :] = returned[levels(c)].astype(F32)
        for t in range(NZ // 2):
            one = chosen[:, :, 2 * t * 128 : (2 * t + 1) * 128].reshape(flat, 128)
            two = chosen[:, :, (2 * t + 1) * 128 : (2 * t + 2) * 128].reshape(flat, 128)
            columns = slice(t * 128, (t + 1) * 128)
            waves[:flat, columns] = jnp.where(even_group, one, pltpu.roll(two, 32, 1)).astype(BF)
            waves[flat:, columns] = jnp.where(even_group, pltpu.roll(one, 96, 1), two).astype(BF)
        both = dot(waves[...], pick[...], 1, 1).astype(BF)
        coded = [
            jnp.concatenate([both[:flat, n : n + HALF], both[flat:, n : n + HALF]], axis=1)
            for n in (0, HALF)
        ]
        for t in range(NLON // 2 // 256):
            rows = slice(t * 256, (t + 1) * 256)
            sums = [dot(coded[parity], table[parity, rows, :], 1, 1) for parity in range(2)]
            low = (2.0 * (sums[0] + sums[1])).reshape(CH, PADR, 256)
            high = (2.0 * (sums[0] - sums[1])).reshape(CH, PADR, 256)
            new_ref[levels(c), :, rows] = low[:, :ROWS].astype(BF)
            new_ref[levels(c), :, NLON // 2 + t * 256 : NLON // 2 + (t + 1) * 256] = high[:, :ROWS].astype(BF)
    for c in range(NCH):
        all_z_back(c).wait_send()


def body(state, panels, pair_table, lat_order, gauss_weights, eig, left, right):
    by_plane = jnp.transpose(lat_order.reshape(NZ, 4, ROWS), (1, 0, 2))
    target = jnp.where(by_plane < HALF, by_plane, HALF + 2 * HALF - 1 - by_plane)
    target = jnp.pad(target, ((0, 0), (0, 0), (0, PADR - ROWS)), constant_values=-1).reshape(1, -1)
    flat = CH * PADR
    wire = (NCH, NS, 4 * CH, NZ * PADR)
    along = (LEVD, NZ, ROWS, 128)
    sems = pltpu.SemaphoreType.DMA((NCH,))
    new_state, spectral = pl.pallas_call(
        step_kernel,
        out_shape=(
            jax.ShapeDtypeStruct((LEVD, ROWS, NLON), BF),
            jax.ShapeDtypeStruct((2, LEV, NCOL), BF),
        ),
        in_specs=[SM] + [pl.BlockSpec(memory_space=pl.ANY)] * 3 + [VM] * 8,
        out_specs=(VM, VM),
        scratch_shapes=[
            pltpu.VMEM((LEVD, ROWS, NLON), BF),
            pltpu.VMEM((HALF, NCOL), BF),
            pltpu.VMEM((2, NCOL, NCOL), BF),
            pltpu.VMEM((NCOL, NZ * 64), BF),
            pltpu.VMEM((NCOL, 4 * NZ * PADR), BF),
            pltpu.VMEM((CH, PADR, NLON), F32),
            pltpu.VMEM((2 * flat, NCOL), BF),
            pltpu.VMEM((LEVD, ROWS, NZ * 128), BF),
            pltpu.VMEM(along, BF),
            pltpu.VMEM((CH, NZ, PADR, 128), F32),
            pltpu.VMEM(wire, BF),
            pltpu.VMEM(wire, BF),
            pltpu.VMEM((NS, 16, NZ * PADR), F32),
            pltpu.VMEM((NCH * 128, NCOL), BF),
            pltpu.VMEM((4 * LEV, NCH * 128), BF),
            pltpu.VMEM((2, LEV, NCH * 128), BF),
            pltpu.VMEM((2, LEV, NCOL), BF),
            pltpu.VMEM((256, HALF), BF),
            pltpu.VMEM((256, NCOL), BF),
            pltpu.VMEM((1, NCOL), F32),
            pltpu.VMEM(wire, BF),
            pltpu.VMEM(wire, BF),
            pltpu.VMEM(along, BF),
            pltpu.VMEM((LEVD, ROWS, NZ * 128), BF),
            pltpu.VMEM((CH, PADR, NZ * 128), F32),
            pltpu.VMEM((2 * flat, NZ * 64), BF),
            pltpu.SemaphoreType.DMA((3 + NCH,)),
            sems, sems, sems, sems,
            pltpu.SemaphoreType.DMA((4 * NCH,)),
            sems, sems, sems, sems,
        ],
        compiler_params=pltpu.CompilerParams(
            collective_id=0, has_side_effects=True, vmem_limit_bytes=LIMIT
        ),
        name="step",
    )(
        pair_table, state, panels, jnp.asarray(dft_table()), pair_table.reshape(4, 128), target, gauss_weights.reshape(1, -1),
        eig.reshape(1, -1), left, right, jnp.asarray(lane_order()), jnp.asarray(level_rows()),
    )
    return new_state, spectral[None]


def solution(mesh):
    return jax.shard_map(
        body,
        mesh=mesh,
        in_specs=(
            P("lev", "wave", None),
            P(("wave", "lev"), None, None),
            P(),
            P(),
            P(),
            P(),
            P(),
            P(),
        ),
        out_specs=(P("lev", "wave", None), P(("wave", "lev"), None, None, None)),
        check_vma=False,
    )
```

```python
import math

import jax
import jax.numpy as jnp
import ml_dtypes
import numpy as np
from jax import lax
from jax.experimental import pallas as pl
from jax.experimental.pallas import tpu as pltpu
from jax.sharding import PartitionSpec as P

NLON = 2560
NCOL = 1280
HALF = 640
LEV = 72
LEVD = 9
ROWS = 20
PADR = 24
NZ = 16
NS = 32
CH = 3
NCH = LEVD // CH
MESH = pl.DeviceIdType.MESH
VM = pl.BlockSpec(memory_space=pltpu.VMEM)
SM = pl.BlockSpec(memory_space=pltpu.SMEM)
F32 = jnp.float32
BF = jnp.bfloat16
LIMIT = 56 * 1024 * 1024


def dft_table():
    x = np.arange(NLON // 2, dtype=np.int64)
    out = []
    for parity in (0, 1):
        m = 2 * np.arange(HALF, dtype=np.int64) + parity
        angle = (x[:, None] * m[None, :] % NLON) * (2.0 * math.pi / NLON)
        both = np.concatenate([np.cos(angle), -np.sin(angle)], axis=1)
        out.append(both * (1.0 / math.sqrt(NLON)))
    return np.stack(out).astype(np.float32).astype(ml_dtypes.bfloat16)


def lane_order():
    e = np.zeros((NS, 16, CH, 2, 2, NS), np.float32)
    for d in range(NS):
        for i in range(CH):
            for ab in range(2):
                for q in range(2):
                    e[d, i * 4 + ab * 2 + q, i, ab, q, d] = 1.0
    return e.reshape(NS * 16, CH * 128).astype(ml_dtypes.bfloat16)


def level_rows():
    o = np.zeros((4, LEV, NCH, 8, 16), np.float32)
    for c in range(NCH):
        for g in range(8):
            for i in range(CH):
                for j in range(4):
                    o[j, g * LEVD + c * CH + i, c, g, i * 4 + j] = 1.0
    return o.reshape(4, LEV, NCH * 128).astype(ml_dtypes.bfloat16)


def row_sources():
    w = np.arange(NZ)[None, :, None] * 4 + np.arange(4)[:, None, None]
    r = np.arange(PADR)[None, None, :]
    return np.where(r < ROWS, w * ROWS + r, -1).reshape(1, -1).astype(np.int32)


def dot(a, b, ca=1, cb=0):
    return lax.dot_general(a, b, (((ca,), (cb,)), ((), ())), preferred_element_type=F32)


def each(count, act):
    def one(k, carry):
        act(k)
        return carry

    lax.fori_loop(1, count, one, 0)


def straight(count, act):
    for k in range(1, count):
        act(k)


def lanes(z):
    return pl.ds(pl.multiple_of(z * 128, 128), 128)


def iota(shape, axis):
    return lax.broadcasted_iota(jnp.int32, shape, axis)


def step_kernel(
    table_pairs, state_hbm, panel_hbm, table_hbm, pairs_ref, lat_ref, source_ref, weight_ref, eig_ref, left_ref, right_ref,
    lane_ref, rows_ref, new_ref, spectral_ref,
    state, panel, table, pick, order, grid, spec, sent, got_z, wide, made, got_p, tall, raw, mix, spread, solved,
    part, masked, scale, target, factor, home, got_q, ready_z, returned, chosen, waves,
    load, zs, zr, ps, pr, own, qs, qr, ys, yr,
):
    wave, group = lax.axis_index("wave"), lax.axis_index("lev")
    z, s = wave // 4, lax.rem(wave, 4)
    me = s * 8 + group
    first = table_pairs[wave * 8 + group]
    flat = CH * PADR

    def along_z(k):
        step = (k + 0) // 2
        other = lax.rem(z + 8 + step * (1 - 2 * lax.rem(k, 2)) + NZ, NZ)
        return other, (other * 4 + s, group)

    def in_plane(k):
        other = lax.rem(me + k, NS)
        return other, (z * 4 + other // 8, lax.rem(other, 8))

    loads = [pltpu.make_async_copy(table_hbm.at[p], table.at[p], load.at[p]) for p in range(2)]
    for c in range(NCH):
        part_of = slice(c * CH, (c + 1) * CH)
        loads.append(pltpu.make_async_copy(state_hbm.at[part_of], state.at[part_of], load.at[2 + c]))
    loads.append(pltpu.make_async_copy(panel_hbm.at[0], panel, load.at[2 + NCH]))
    for n in (2, 0, 1, 3, 4, 5):
        loads[n].start()

    barrier = pltpu.get_barrier_semaphore()

    def hail(of):
        def act(k):
            pl.semaphore_signal(barrier, inc=1, device_id=of(k)[1], device_id_type=MESH)

        return act

    each(NZ, hail(along_z))
    each(NS, hail(in_plane))

    def remote(src, dst, send, recv, device):
        return pltpu.make_async_remote_copy(
            src_ref=src, dst_ref=dst, send_sem=send, recv_sem=recv, device_id=device, device_id_type=MESH
        )

    def levels(c):
        return slice(c * CH, (c + 1) * CH)

    def z_out(c, k):
        other, device = along_z(k)
        return remote(sent.at[levels(c), :, lanes(other)], got_z.at[levels(c), z], zs.at[c], zr.at[c], device)

    def p_out(c, k):
        other, device = in_plane(k)
        return remote(made.at[c, other], got_p.at[c, me], ps.at[c], pr.at[c], device)

    def p_back(c, k):
        other, device = in_plane(k)
        return remote(home.at[c, other], got_q.at[c, me], qs.at[c], qr.at[c], device)

    def z_back(c, k):
        other, device = along_z(k)
        return remote(ready_z.at[levels(c), other], returned.at[levels(c), :, lanes(z)], ys.at[c], yr.at[c], device)

    def whole(ref, send, recv, device):
        return remote(ref, ref, send, recv, device)

    def all_z_out(c):
        return whole(got_z.at[levels(c), : NZ - 1], zs.at[c], zr.at[c], along_z(1)[1])

    def all_p_out(c):
        return whole(got_p.at[c, : NS - 1], ps.at[c], pr.at[c], in_plane(1)[1])

    def all_p_back(c):
        return whole(got_q.at[c, : NS - 1], qs.at[c], qr.at[c], in_plane(1)[1])

    def all_z_back(c):
        return whole(ready_z.at[levels(c), : NZ - 1], ys.at[c], yr.at[c], along_z(1)[1])

    lane = iota((8, 128), 1)
    for t in range(NZ // 2):
        here = jnp.broadcast_to(pairs_ref[t // 2 : t // 2 + 1, :], (8, 128))
        there = pltpu.roll(here, 64, 1)
        low, high = (here, there) if t % 2 == 0 else (there, here)
        number = jnp.where(lane < 64, low, NCOL - high)
        pos = (lax.rem(number, 2) * HALF + lax.shift_right_logical(number, 1))[:1]
        pick[:, t * 128 : (t + 1) * 128] = (iota((NCOL, 128), 0) == pos).astype(F32).astype(BF)
    grid[...] = jnp.zeros_like(grid)
    wide[...] = jnp.zeros_like(wide)
    tall[...] = jnp.zeros_like(tall)
    chosen[...] = jnp.zeros_like(chosen)
    even_group = lax.rem(iota((flat, 128), 1) // 32, 2) == 0

    mine = []
    for c in range(NCH):
        loads[2 + c].wait()
        grid[:, :ROWS, :] = state[levels(c)].astype(F32)
        low = grid[:, :, : NLON // 2].reshape(flat, NLON // 2)
        high = grid[:, :, NLON // 2 :].reshape(flat, NLON // 2)
        for parity, half in ((0, low + high), (1, low - high)):
            if c == 0:
                loads[parity].wait()
            both = dot(half.astype(BF), table[parity]).astype(BF)
            spec[:flat, parity * HALF : (parity + 1) * HALF] = both[:, :HALF]
            spec[flat:, parity * HALF : (parity + 1) * HALF] = both[:, HALF:]
        for t in range(NZ // 2):
            got = dot(spec[...], pick[:, t * 128 : (t + 1) * 128])
            cos, sin = got[:flat], got[flat:]
            one = jnp.where(even_group, cos, pltpu.roll(sin, 32, 1))
            two = jnp.where(even_group, pltpu.roll(cos, 96, 1), sin)
            for h, value in ((0, one), (1, two)):
                columns = slice((2 * t + h) * 128, (2 * t + h + 1) * 128)
                sent[levels(c), :, columns] = value.reshape(CH, PADR, 128)[:, :ROWS].astype(BF)
        if c == 0:
            pl.semaphore_wait(barrier, NZ - 1 + NS - 1)
        (straight if c == 0 else each)(NZ, lambda k: z_out(c, k).start())
        copy = pltpu.make_async_copy(sent.at[levels(c), :, lanes(z)], got_z.at[levels(c), z], own.at[c])
        copy.start()
        mine.append(copy)

    for t in range(NCOL // 128):
        scale[:, t * 128 : (t + 1) * 128] = weight_ref[t : t + 1, :]
    kind = iota((8, 128), 0)
    parts = jnp.zeros((8, 4 * NZ * PADR), F32)
    for t in range(NCOL // 128):
        lat = jnp.broadcast_to(lat_ref[t : t + 1, :], (8, 128))
        short = jnp.where(kind == 0, lax.shift_right_logical(lat, 4), lax.rem(lat, 16))
        places = (iota((128, 4 * NZ * PADR), 0) + t * 128 == source_ref[...]).astype(F32).astype(BF)
        parts += dot(short.astype(F32).astype(BF), places)
    lat = (16.0 * parts[0:1] + parts[1:2]).astype(jnp.int32)
    lat = jnp.where(lat < HALF, lat, HALF + 2 * HALF - 1 - lat)
    target[...] = jnp.where(source_ref[...] < 0, -1, lat)

    def build(t, carry):
        rows = pl.ds(pl.multiple_of(t * 128, 128), 128)
        order[rows, :] = (iota((128, 4 * NZ * PADR), 0) + t * 128 == target[...]).astype(F32).astype(BF)
        return carry

    lax.fori_loop(0, NCOL // 128, build, 0)
    for j in range(4):
        mix[j * LEV : (j + 1) * LEV, :] = dot(right_ref[...], rows_ref[j]).astype(BF)
    for q in range(2):
        spread[q] = (rows_ref[q].astype(F32) + rows_ref[q + 2].astype(F32)).astype(BF)
    eig = jnp.sum(
        jnp.where(iota((LEV, LEV), 0) == iota((LEV, LEV), 1), eig_ref[...], 0.0), axis=1, keepdims=True
    )

    row, column = iota((HALF, HALF), 0), iota((HALF, HALF), 1)
    south = jnp.where(row + column == HALF - 1, scale[:, HALF:], 0.0)
    south = jnp.where(row == column, jnp.sum(south, axis=1, keepdims=True), 0.0)
    scale[:, HALF:] = jnp.sum(south, axis=0, keepdims=True)

    def column_facts(start, width):
        column = iota((1, width), 1) + start
        owned = column < NCOL - first
        shifted = jnp.where(owned, column, column + first)
        mirror = jnp.where(lax.rem(shifted, 2) == 0, 1.0, -1.0).astype(F32)
        return column, owned, mirror

    column, owned, _ = column_facts(0, NCOL)
    degree = jnp.where(owned, column + first, column).astype(F32)
    factor[...] = 1.0 / (1.0 + degree * (degree + 1.0) / (NCOL * (NCOL - 1.0)) * eig)

    def turn(c):
        mine[c].wait()
        all_z_out(c).wait_recv()
        for i in range(CH):
            wide[i, :, :ROWS, :] = got_z[c * CH + i].astype(F32)
        block = jnp.concatenate(
            [wide[i].reshape(NZ * PADR, 128).astype(BF) for i in range(CH)], axis=1
        )
        value = dot(lane_ref[...], block, 1, 1).reshape(NS, 16, NZ * PADR)
        made[c] = value[:, : 4 * CH].astype(BF)
        (straight if c == NCH - 1 else each)(NS, lambda k: p_out(c, k).start())
        copy = pltpu.make_async_copy(made.at[c, me], got_p.at[c, me], own.at[NCH + c])
        copy.start()
        return copy

    def legendre(c, copy):
        copy.wait()
        all_p_out(c).wait_recv()
        tall[:, : 4 * CH, :] = got_p[c].astype(F32)
        block = jnp.concatenate(
            [tall[b * 8 : (b + 1) * 8].reshape(128, NZ * PADR).astype(BF) for b in range(4)], axis=1
        )
        value = dot(block, order[...], 1, 1)
        weighted = (value * scale[...]).astype(BF)
        part[:128] = weighted[:, :HALF]
        part[128:] = weighted[:, HALF:]
        mirror = column_facts(0, NCOL)[2]
        both = dot(part[...], panel[...])
        raw[c * 128 : (c + 1) * 128, :] = (both[:128] + mirror * both[128:]).astype(BF)

    copies = [turn(0), turn(1)]
    loads[2 + NCH].wait()
    legendre(0, copies[0])
    copies.append(turn(2))
    legendre(1, copies[1])
    legendre(2, copies[2])

    owned = column_facts(0, NCOL)[1]
    for t in range(NCOL // 256):
        columns = slice(t * 256, (t + 1) * 256)
        mixed = dot(mix[...], raw[:, columns])
        for q in range(2):
            upper = mixed[q * LEV : (q + 1) * LEV]
            lower = mixed[(q + 2) * LEV : (q + 3) * LEV]
            scaled = (jnp.where(owned[:, columns], upper, lower) * factor[:, columns]).astype(BF)
            value = dot(left_ref[...], scaled).astype(BF)
            solved[q, :, columns] = value
            spectral_ref[q, :, columns] = value

    def leave(c):
        _, owned, mirror = column_facts(0, NCOL)
        value = dot(spread[0, :, c * 128 : (c + 1) * 128], solved[0], 0, 0)
        value += dot(spread[1, :, c * 128 : (c + 1) * 128], solved[1], 0, 0)
        kept = jnp.where((lax.rem(iota((128, NCOL), 0), 4) < 2) == owned, value, 0.0)
        masked[:128] = kept.astype(BF)
        masked[128:] = (kept * mirror).astype(BF)
        both = dot(masked[...], panel[...], 1, 1).astype(BF)
        by_lat = jnp.concatenate([both[:128], both[128:]], axis=1)
        for b in range(4):
            value = dot(by_lat, order[:, b * 384 : (b + 1) * 384])
            home[c, b * 8 : (b + 1) * 8] = value.reshape(8, 16, NZ * PADR)[:, : 4 * CH].astype(BF)
        (straight if c == 0 else each)(NS, lambda k: p_back(c, k).start())
        copy = pltpu.make_async_copy(home.at[c, me], got_q.at[c, me], own.at[2 * NCH + c])
        copy.start()
        return copy

    def retrace(c, arrived):
        arrived.wait()
        all_p_back(c).wait_recv()
        tall[:, : 4 * CH, :] = got_q[c].astype(F32)
        value = dot(tall[...].reshape(NS * 16, NZ * PADR).astype(BF), lane_ref[...], 0, 0)
        for i in range(CH):
            block = value[:, i * 128 : (i + 1) * 128].reshape(NZ, PADR, 128)
            ready_z[c * CH + i] = block[:, :ROWS].astype(BF)
        (straight if c == 0 else each)(NZ, lambda k: z_back(c, k).start())
        copy = pltpu.make_async_copy(ready_z.at[levels(c), z], returned.at[levels(c), :, lanes(z)], own.at[3 * NCH + c])
        copy.start()
        return copy

    homes = [leave(0), leave(1)]
    lasts = [retrace(0, homes[0])]
    homes.append(leave(2))
    lasts += [retrace(1, homes[1]), retrace(2, homes[2])]
    for c in range(NCH):
        all_z_out(c).wait_send()
        all_p_out(c).wait_send()
        all_p_back(c).wait_send()

    for c in range(NCH):
        lasts[c].wait()
        all_z_back(c).wait_recv()
        chosen[:, :ROWS, :] = returned[levels(c)].astype(F32)
        for t in range(NZ // 2):
            one = chosen[:, :, 2 * t * 128 : (2 * t + 1) * 128].reshape(flat, 128)
            two = chosen[:, :, (2 * t + 1) * 128 : (2 * t + 2) * 128].reshape(flat, 128)
            columns = slice(t * 128, (t + 1) * 128)
            waves[:flat, columns] = jnp.where(even_group, one, pltpu.roll(two, 32, 1)).astype(BF)
            waves[flat:, columns] = jnp.where(even_group, pltpu.roll(one, 96, 1), two).astype(BF)
        both = dot(waves[...], pick[...], 1, 1).astype(BF)
        coded = [
            jnp.concatenate([both[:flat, n : n + HALF], both[flat:, n : n + HALF]], axis=1)
            for n in (0, HALF)
        ]
        for t in range(NLON // 2 // 256):
            rows = slice(t * 256, (t + 1) * 256)
            sums = [dot(coded[parity], table[parity, rows, :], 1, 1) for parity in range(2)]
            low = (2.0 * (sums[0] + sums[1])).reshape(CH, PADR, 256)
            high = (2.0 * (sums[0] - sums[1])).reshape(CH, PADR, 256)
            new_ref[levels(c), :, rows] = low[:, :ROWS].astype(BF)
            new_ref[levels(c), :, NLON // 2 + t * 256 : NLON // 2 + (t + 1) * 256] = high[:, :ROWS].astype(BF)
    for c in range(NCH):
        all_z_back(c).wait_send()


def body(state, panels, pair_table, lat_order, gauss_weights, eig, left, right):
    flat = CH * PADR
    wire = (NCH, NS, 4 * CH, NZ * PADR)
    along = (LEVD, NZ, ROWS, 128)
    sems = pltpu.SemaphoreType.DMA((NCH,))
    new_state, spectral = pl.pallas_call(
        step_kernel,
        out_shape=(
            jax.ShapeDtypeStruct((LEVD, ROWS, NLON), BF),
            jax.ShapeDtypeStruct((2, LEV, NCOL), BF),
        ),
        in_specs=[SM] + [pl.BlockSpec(memory_space=pl.ANY)] * 3 + [VM] * 9,
        out_specs=(VM, VM),
        scratch_shapes=[
            pltpu.VMEM((LEVD, ROWS, NLON), BF),
            pltpu.VMEM((HALF, NCOL), BF),
            pltpu.VMEM((2, NCOL, NCOL), BF),
            pltpu.VMEM((NCOL, NZ * 64), BF),
            pltpu.VMEM((NCOL, 4 * NZ * PADR), BF),
            pltpu.VMEM((CH, PADR, NLON), F32),
            pltpu.VMEM((2 * flat, NCOL), BF),
            pltpu.VMEM((LEVD, ROWS, NZ * 128), BF),
            pltpu.VMEM(along, BF),
            pltpu.VMEM((CH, NZ, PADR, 128), F32),
            pltpu.VMEM(wire, BF),
            pltpu.VMEM(wire, BF),
            pltpu.VMEM((NS, 16, NZ * PADR), F32),
            pltpu.VMEM((NCH * 128, NCOL), BF),
            pltpu.VMEM((4 * LEV, NCH * 128), BF),
            pltpu.VMEM((2, LEV, NCH * 128), BF),
            pltpu.VMEM((2, LEV, NCOL), BF),
            pltpu.VMEM((256, HALF), BF),
            pltpu.VMEM((256, NCOL), BF),
            pltpu.VMEM((1, NCOL), F32),
            pltpu.VMEM((1, 4 * NZ * PADR), jnp.int32),
            pltpu.VMEM((LEV, NCOL), F32),
            pltpu.VMEM(wire, BF),
            pltpu.VMEM(wire, BF),
            pltpu.VMEM(along, BF),
            pltpu.VMEM((LEVD, ROWS, NZ * 128), BF),
            pltpu.VMEM((CH, PADR, NZ * 128), F32),
            pltpu.VMEM((2 * flat, NZ * 64), BF),
            pltpu.SemaphoreType.DMA((3 + NCH,)),
            sems, sems, sems, sems,
            pltpu.SemaphoreType.DMA((4 * NCH,)),
            sems, sems, sems, sems,
        ],
        compiler_params=pltpu.CompilerParams(
            collective_id=0, has_side_effects=True, vmem_limit_bytes=LIMIT
        ),
        name="step",
    )(
        pair_table, state, panels, jnp.asarray(dft_table()), pair_table.reshape(4, 128),
        lat_order.reshape(-1, 128), jnp.asarray(row_sources()), gauss_weights.reshape(-1, 128),
        eig.reshape(1, -1), left, right, jnp.asarray(lane_order()), jnp.asarray(level_rows()),
    )
    return new_state, spectral[None]


def solution(mesh):
    return jax.shard_map(
        body,
        mesh=mesh,
        in_specs=(
            P("lev", "wave", None),
            P(("wave", "lev"), None, None),
            P(),
            P(),
            P(),
            P(),
            P(),
            P(),
        ),
        out_specs=(P("lev", "wave", None), P(("wave", "lev"), None, None, None)),
        check_vma=False,
    )
```
